128 devices in a mesh: edata: 8 (over y, x_hi), tensor: 16 (over z, x_lo, core).
Axes of the slice: x: 4 (x_hi: 2, x_lo: 2; x = x_hi * 2 + x_lo), y: 4, z: 4, core: 2. Of those that a mesh axis runs over, the one named last changes fastest.
Arguments:
- tokens: bfloat16 [2048, 6144], P('tensor', 'edata'), may hold values from -6 to 6
- expert_ids: int32 [2048, 2], P('tensor'), may hold values from 0 to 7, as said below
- route_weight: float32 [2048, 2], P('tensor'), may hold values from 0.25 to 1
- up_weight: bfloat16 [2, 6144, 16384], P(None, 'edata', 'tensor'), may hold values from -0.078125 to 0.078125
- down_weight: bfloat16 [2, 16384, 6144], P(None, 'tensor', 'edata'), may hold values from -0.046875 to 0.046875
- target_up: bfloat16 [2, 6144, 16384], P(None, 'edata', 'tensor'), may hold values from -0.078125 to 0.078125
- target_down: bfloat16 [2, 16384, 6144], P(None, 'tensor', 'edata'), may hold values from -0.046875 to 0.046875
- cotangent: bfloat16 [2048, 6144], P('tensor', 'edata'), may hold values from -6 to 6
Outputs:
- mixed: bfloat16 [2048, 6144], P('tensor', 'edata')
- grad_tokens: bfloat16 [2048, 6144], P('tensor', 'edata')
- grad_up: bfloat16 [2, 6144, 16384], P(None, 'edata', 'tensor')
- grad_down: bfloat16 [2, 16384, 6144], P(None, 'tensor', 'edata')
- target_mixed: bfloat16 [2048, 6144], P('tensor', 'edata')
The draws below stay inside these ranges and needn't reach their ends.
Inputs may be any that keep to these rules, and one draw needn't show every extreme that they name: `expert_ids`: every token names 2 different experts. Among the 128 tokens of one tensor index no expert is named by more than 48 tokens, and expert 0 is named by exactly 48.
All inputs are finite; a program needn't handle non-finite values.
Results may differ from the reference program's by a relative error of at most 0.03.
Values may be sent and summed in bfloat16 or wider, within the bound.
No kernel may reach another device: no remote copies, remote signals or barrier semaphores. Data moves between devices by JAX's collectives and lax.ppermute only.
A program may use at most 128 MiB of HBM per device.

```python
import math
import jax
import jax.numpy as jnp
from jax import lax

D = 6144
FF = 16384
EXPERTS = 8
TOPK = 2
EXP_WIN = 2
TOK_DEV = 128
CAP = 48
TOKENS = 2048
ROUTED = 768
N_EDATA = 8
N_TENSOR = 16


def draw_expert_ids(key, part):
    block_count = TOKENS // TOK_DEV

    def one_block(block_key):
        first_key, second_key, third_key, fourth_key = jax.random.split(block_key, 4)
        second_count = jax.random.randint(first_key, (), 1, CAP + 1)
        remaining = 2 * TOK_DEV - CAP - second_count
        portion = jax.random.randint(second_key, (EXPERTS - 2,), 3, 5)
        counts_rest = remaining * portion // jnp.sum(portion)
        leftover = remaining - jnp.sum(counts_rest)
        counts_rest = counts_rest + (jnp.arange(EXPERTS - 2) < leftover).astype(jnp.int32)
        counts = jnp.concatenate([jnp.array([CAP], jnp.int32), second_count[None].astype(jnp.int32), counts_rest.astype(jnp.int32)])
        listed = jnp.repeat(jnp.arange(EXPERTS, dtype=jnp.int32), counts, total_repeat_length=2 * TOK_DEV)
        paired = jnp.stack([listed[:TOK_DEV], listed[TOK_DEV:]], axis=1)
        swapped = jax.random.randint(third_key, (TOK_DEV, 1), 0, 2)
        paired = jnp.where(swapped == 1, paired[:, ::-1], paired)
        shuffle = jax.random.permutation(fourth_key, TOK_DEV)
        return paired[shuffle]
    block_keys = jax.random.split(key, block_count)
    return jax.vmap(one_block)(block_keys).reshape(TOKENS, TOPK).astype(jnp.int32)


def block_levels(key, dims, cuts, low, high):
    level = 1.0
    for dim, shards_of in cuts:
        draws = jax.random.uniform(jax.random.fold_in(jax.random.fold_in(key, 6), dim), (shards_of,), jnp.float32, low / len(cuts), high / len(cuts))
        level = level * jnp.repeat(jnp.exp(draws), dims[dim] // shards_of).reshape((-1,) + (1,) * (len(dims) - 1 - dim))
    return level


def scatter_about(stream_key, extent, scale, most, cuts=(), kind=jnp.bfloat16):
    entries = jax.random.normal(stream_key, extent, jnp.float32) * scale
    if len(cuts) > 0:
        entries = block_levels(stream_key, extent, cuts, -0.22, 0.18) * entries
    return jnp.clip(entries, min=-most, max=most).astype(kind)


def setup_inputs(seed: int = 0) -> dict:
    seeds = jax.random.split(jax.random.key(seed), 9)
    return {
        "tokens": scatter_about(seeds[0], (TOKENS, D), 1.0, 6.0, ((0, 16), (1, 8))),
        "expert_ids": draw_expert_ids(jax.random.fold_in(seeds[8], 71), 0),
        "route_weight": jnp.clip(jnp.exp(math.log(1.0) - 1.3862944 * jax.random.uniform(seeds[2], (TOKENS, TOPK), jnp.float32) ** block_levels(seeds[2], (TOKENS, TOPK), ((0, 16),), -0.2, 0.2)), 0.25, 1.0),
        "up_weight": scatter_about(seeds[3], (EXP_WIN, D, FF), D ** -0.5, 0.078125, ((1, 8), (2, 16))),
        "down_weight": scatter_about(seeds[4], (EXP_WIN, FF, D), FF ** -0.5, 0.046875, ((1, 16), (2, 8))),
        "target_up": scatter_about(seeds[5], (EXP_WIN, D, FF), D ** -0.5, 0.078125, ((1, 8), (2, 16))),
        "target_down": scatter_about(seeds[6], (EXP_WIN, FF, D), FF ** -0.5, 0.046875, ((1, 16), (2, 8))),
        "cotangent": scatter_about(seeds[7], (TOKENS, D), 1.0, 6.0, ((0, 16), (1, 8))),
    }


def group_tables(expert_ids, route_weight):
    id_rows = expert_ids.reshape(N_TENSOR, TOK_DEV, TOPK)
    route_rows = route_weight.reshape(N_TENSOR, TOK_DEV, TOPK)
    owner_row = jnp.arange(N_TENSOR, dtype=jnp.int32)[:, None] * jnp.ones((1, TOK_DEV), jnp.int32)
    within = jnp.ones((N_TENSOR, 1), jnp.int32) * jnp.arange(TOK_DEV, dtype=jnp.int32)[None, :]
    token_index = (owner_row * TOK_DEV + within).astype(jnp.int32)
    sources, portions, valids = [], [], []
    for expert in range(EXP_WIN):
        chosen = id_rows == expert
        listed = jnp.any(chosen, axis=2)
        position = jnp.cumsum(listed.astype(jnp.int32), axis=1) - 1
        placed = jnp.where(listed, position, CAP).astype(jnp.int32)
        source = jnp.zeros((N_TENSOR, CAP + 1), jnp.int32).at[owner_row, placed].set(token_index)[:, :CAP]
        weight = jnp.sum(jnp.where(chosen, route_rows, jnp.float32(0.0)), axis=2)
        portion = jnp.zeros((N_TENSOR, CAP + 1), jnp.float32).at[owner_row, placed].set(weight)[:, :CAP]
        valid = jnp.zeros((N_TENSOR, CAP + 1), jnp.int32).at[owner_row, placed].set(1)[:, :CAP]
        sources.append(source.reshape(ROUTED))
        portions.append(portion.reshape(ROUTED))
        valids.append(valid.reshape(ROUTED))
    return jnp.stack(sources), jnp.stack(portions), jnp.stack(valids)


def blocked(matrix, factor, pieces):
    span_size = matrix.shape[1] // pieces
    running = jnp.zeros((matrix.shape[0], factor.shape[1]), jnp.float32)
    for piece in range(pieces):
        partial_value = jnp.dot(matrix[:, piece * span_size:(piece + 1) * span_size],
                          factor[piece * span_size:(piece + 1) * span_size],
                          preferred_element_type=jnp.float32)
        rounded = lax.optimization_barrier(partial_value.astype(jnp.bfloat16))
        running = running + rounded.astype(jnp.float32)
    return running


def forward(routed_rows, up_matrix, down_matrix):
    hidden_pre = blocked(routed_rows, up_matrix, N_EDATA)
    active = jax.nn.silu(hidden_pre).astype(jnp.bfloat16)
    summed = jnp.dot(active, down_matrix, preferred_element_type=jnp.float32)
    return hidden_pre, active, summed


def combine_back(results, source, portion):
    weighted = portion[:, :, None] * results
    running = jnp.zeros((TOKENS, D), jnp.float32)
    running = running.at[source.reshape(-1)].add(weighted.reshape(-1, D))
    return running.astype(jnp.bfloat16)


def reference(tokens, expert_ids, route_weight, up_weight, down_weight, target_up, target_down, cotangent):
    source, portion, valid = group_tables(expert_ids, route_weight)
    routed_tokens = jnp.where(valid[:, :, None] > 0, tokens[source], jnp.zeros((), tokens.dtype)).astype(jnp.bfloat16)
    routed_grad = (portion[:, :, None] * cotangent[source].astype(jnp.float32)).astype(jnp.bfloat16)
    online_list, target_list, grad_rows_list, grad_up_list, grad_down_list = [], [], [], [], []
    for expert in range(EXP_WIN):
        hidden_pre, active, summed = forward(routed_tokens[expert], up_weight[expert], down_weight[expert])
        online_list.append(summed)
        grad_down_list.append(jnp.dot(active.T, routed_grad[expert], preferred_element_type=jnp.float32).astype(jnp.bfloat16))
        grad_active = blocked(routed_grad[expert], down_weight[expert].T, N_EDATA)
        logistic = jax.nn.sigmoid(hidden_pre)
        grad_pre = (grad_active * logistic * (1.0 + hidden_pre * (1.0 - logistic))).astype(jnp.bfloat16)
        grad_up_list.append(jnp.dot(routed_tokens[expert].T, grad_pre, preferred_element_type=jnp.float32).astype(jnp.bfloat16))
        grad_rows_list.append(jnp.dot(grad_pre, up_weight[expert].T, preferred_element_type=jnp.float32))
        blended_up = (0.75 * target_up[expert].astype(jnp.float32) + 0.25 * up_weight[expert].astype(jnp.float32)).astype(jnp.bfloat16)
        blended_down = (0.75 * target_down[expert].astype(jnp.float32) + 0.25 * down_weight[expert].astype(jnp.float32)).astype(jnp.bfloat16)
        target_pre, target_active, target_out = forward(routed_tokens[expert], blended_up, blended_down)
        target_list.append(target_out)
    mixed = combine_back(jnp.stack(online_list), source, portion)
    grad_tokens = combine_back(jnp.stack(grad_rows_list), source, portion)
    target_mixed = combine_back(jnp.stack(target_list), source, portion)
    return mixed, grad_tokens, jnp.stack(grad_up_list), jnp.stack(grad_down_list), target_mixed
```

```python
import jax
import jax.numpy as jnp
from jax import lax
from jax.sharding import PartitionSpec as P

EXP_WIN = 2
CAP = 48

EDATA_MASK = {"a": 2, "b": 6, "c": 1}
TENSOR_MASK = {"l": 2, "z1": 4, "z3": 12, "k": 1}
DIM = {"k": 0, "z3": 1, "z1": 2, "l": 3}
SPLIT = {"a": "l", "b": "z1", "c": "z3"}
ORDERS = {
    ("pre", 0): "abc",
    ("pre", 1): "bca",
    ("target", 0): "cab",
    ("grad", 0): "abc",
    ("grad", 1): "bca",
    ("target", 1): "cab",
}


def swap(x, axis, mask):
    n = lax.axis_size(axis)
    return lax.ppermute(x, axis, [(i, i ^ mask) for i in range(n)])


def tables(expert_ids, route_weight):
    placed_list, portion_list = ([], [])
    for expert in range(EXP_WIN):
        chosen = expert_ids == expert
        listed = jnp.any(chosen, axis=1)
        position = jnp.cumsum(listed.astype(jnp.int32)) - 1
        placed = (position[None, :] == jnp.arange(CAP, dtype=jnp.int32)[:, None]) & listed[None, :]
        weight = jnp.sum(jnp.where(chosen, route_weight, 0.0), axis=1)
        placed_list.append(placed)
        portion_list.append(jnp.where(placed, weight[None, :], 0.0))
    onehot = jnp.stack(placed_list, axis=0).astype(jnp.bfloat16)
    combine = jnp.stack(portion_list, axis=0)
    return (onehot, combine)


def combined(owner_out, combine):
    return jnp.einsum("ecd,ect->td", owner_out, combine, precision=lax.Precision.HIGHEST).astype(
        jnp.bfloat16
    )


def half(x, dim, index):
    return lax.index_in_dim(x, index, dim, keepdims=True)


def shards(
    tokens, expert_ids, route_weight, up_weight, down_weight, target_up, target_down, cotangent
):
    f32, bf16 = jnp.float32, jnp.bfloat16
    index = lax.axis_index("edata")
    y, x_hi = index // 2, index % 2
    flip = {"l": ((y ^ (y // 2)) & 1) == 1, "z1": y // 2 == 1, "z3": x_hi == 1}

    onehot, combine = tables(expert_ids, route_weight)
    picked = jnp.einsum("ect,td->ecd", onehot, tokens, preferred_element_type=f32).astype(bf16)
    scaled = jnp.einsum(
        "ect,td->ecd", combine, cotangent.astype(f32), precision=lax.Precision.HIGHEST
    ).astype(bf16)

    def gather_rows(rows, order):
        held = rows.reshape((EXP_WIN, 1, 1, 1, 1) + rows.shape[1:])
        for name in order:
            other = swap(held, "tensor", TENSOR_MASK[name])
            dim = DIM[name] + 1
            if name in flip:
                first = jnp.where(flip[name], other, held)
                second = jnp.where(flip[name], held, other)
            else:
                first, second = held, other
            held = jnp.concatenate([first, second], axis=dim)
        return held

    def scatter_rows(rows, order):
        held = rows
        for place, name in enumerate(order):
            dim = DIM[name] + 1
            low, high = half(held, dim, 0), half(held, dim, 1)
            if name in flip:
                keep = jnp.where(flip[name], high, low)
                send = jnp.where(flip[name], low, high)
            else:
                keep, send = low, high
            held = keep.astype(f32) + swap(send.astype(bf16), "tensor", TENSOR_MASK[name]).astype(
                f32
            )
        return held.reshape((EXP_WIN,) + rows.shape[-2:])

    x_rows = gather_rows(picked, ["l", "z1", "z3", "k"])
    g_rows = gather_rows(scaled, ["l", "z3", "z1", "k"])

    def matmul(rows, weight, dims):
        return lax.dot_general(
            rows, weight, (((rows.ndim - 1,), (dims,)), ((), ())), preferred_element_type=f32
        )

    def edata_sum(rows, weight, dims, order):
        first = DIM[SPLIT[order[0]]]
        send = matmul(half(rows, first, 1), weight, dims).astype(bf16)
        other = swap(send, "edata", EDATA_MASK[order[0]])
        held = matmul(half(rows, first, 0), weight, dims).astype(bf16).astype(f32) + other.astype(
            f32
        )
        for name in order[1:]:
            dim = DIM[SPLIT[name]]
            other = swap(half(held, dim, 1).astype(bf16), "edata", EDATA_MASK[name])
            held = half(held, dim, 0) + other.astype(f32)
        return held

    def edata_gather(share, order):
        held = share
        for name in reversed(order):
            other = swap(held, "edata", EDATA_MASK[name])
            held = jnp.concatenate([held, other], axis=DIM[SPLIT[name]])
        return held

    blend_up = (0.75 * target_up.astype(f32) + 0.25 * up_weight.astype(f32)).astype(bf16)
    blend_down = (0.75 * target_down.astype(f32) + 0.25 * down_weight.astype(f32)).astype(bf16)

    pre, grad, target = {}, {}, {}
    for e in range(EXP_WIN):
        pre[e] = edata_sum(x_rows[e], up_weight[e], 0, ORDERS["pre", e])
    for e in range(EXP_WIN):
        grad[e] = edata_sum(g_rows[e], down_weight[e], 1, ORDERS["grad", e])
    for e in range(EXP_WIN):
        target[e] = edata_sum(x_rows[e], blend_up[e], 0, ORDERS["target", e])

    active, grad_pre, target_active = {}, {}, {}
    for e in range(EXP_WIN):
        active[e] = edata_gather(jax.nn.silu(pre[e]).astype(bf16), ORDERS["pre", e])
    for e in range(EXP_WIN):
        logistic = jax.nn.sigmoid(pre[e])
        value = (grad[e] * logistic * (1.0 + pre[e] * (1.0 - logistic))).astype(bf16)
        grad_pre[e] = edata_gather(value, ORDERS["grad", e])
    for e in range(EXP_WIN):
        target_active[e] = edata_gather(jax.nn.silu(target[e]).astype(bf16), ORDERS["target", e])

    def outputs(rows, weight, dims, order):
        out = jnp.stack([matmul(rows[e], weight[e], dims).astype(bf16) for e in range(EXP_WIN)])
        return combined(scatter_rows(out, order), combine)

    def weight_grad(left, right):
        def one(lhs, rhs):
            lhs = lhs.reshape(-1, lhs.shape[-1])
            rhs = rhs.reshape(-1, rhs.shape[-1])
            return lax.dot_general(
                lhs, rhs, (((0,), (0,)), ((), ())), preferred_element_type=f32
            ).astype(bf16)

        return jnp.stack([one(left[e], right[e]) for e in range(EXP_WIN)])

    mixed = outputs(active, down_weight, 0, ["k", "z3", "z1", "l"])
    grad_tokens = outputs(grad_pre, up_weight, 1, ["k", "z1", "z3", "l"])
    target_mixed = outputs(target_active, blend_down, 0, ["k", "z3", "z1", "l"])
    grad_down = weight_grad(active, g_rows)
    grad_up = weight_grad(x_rows, grad_pre)
    return (mixed, grad_tokens, grad_up, grad_down, target_mixed)


def solution(mesh):
    return jax.shard_map(
        shards,
        mesh=mesh,
        in_specs=(
            P("tensor", "edata"),
            P("tensor", None),
            P("tensor", None),
            P(None, "edata", "tensor"),
            P(None, "tensor", "edata"),
            P(None, "edata", "tensor"),
            P(None, "tensor", "edata"),
            P("tensor", "edata"),
        ),
        out_specs=(
            P("tensor", "edata"),
            P("tensor", "edata"),
            P(None, "edata", "tensor"),
            P(None, "tensor", "edata"),
            P("tensor", "edata"),
        ),
        check_vma=False,
    )
```

```python
import jax
import jax.numpy as jnp
from jax import lax
from jax.sharding import PartitionSpec as P

EXP_WIN = 2
CAP = 48

EDATA_MASK = {"a": 2, "b": 6, "c": 1}
TENSOR_MASK = {"l": 2, "z1": 4, "z3": 12, "k": 1}
DIM = {"k": 0, "z3": 1, "z1": 2, "l": 3}
SPLIT = {"a": "l", "b": "z1", "c": "z3"}
ORDERS = {
    ("pre", 0): "abc",
    ("pre", 1): "bca",
    ("target", 0): "cab",
    ("grad", 0): "abc",
    ("grad", 1): "bca",
    ("target", 1): "cab",
}


def swap(x, axis, mask):
    n = lax.axis_size(axis)
    return lax.ppermute(x, axis, [(i, i ^ mask) for i in range(n)])


def tables(expert_ids, route_weight):
    placed_list, portion_list = ([], [])
    for expert in range(EXP_WIN):
        chosen = expert_ids == expert
        listed = jnp.any(chosen, axis=1)
        position = jnp.cumsum(listed.astype(jnp.int32)) - 1
        placed = (position[None, :] == jnp.arange(CAP, dtype=jnp.int32)[:, None]) & listed[None, :]
        weight = jnp.sum(jnp.where(chosen, route_weight, 0.0), axis=1)
        placed_list.append(placed)
        portion_list.append(jnp.where(placed, weight[None, :], 0.0))
    onehot = jnp.stack(placed_list, axis=0).astype(jnp.bfloat16)
    combine = jnp.stack(portion_list, axis=0)
    return (onehot, combine)


def combined(owner_out, combine):
    return jnp.einsum("ecd,ect->td", owner_out, combine, precision=lax.Precision.HIGHEST).astype(
        jnp.bfloat16
    )


def half(x, dim, index):
    return lax.index_in_dim(x, index, dim, keepdims=True)


def shards(
    tokens, expert_ids, route_weight, up_weight, down_weight, target_up, target_down, cotangent
):
    f32, bf16 = jnp.float32, jnp.bfloat16
    index = lax.axis_index("edata")
    y, x_hi = index // 2, index % 2
    flip = {"l": ((y ^ (y // 2)) & 1) == 1, "z1": y // 2 == 1, "z3": x_hi == 1}

    onehot, combine = tables(expert_ids, route_weight)
    picked = jnp.einsum("ect,td->ecd", onehot, tokens, preferred_element_type=f32).astype(bf16)
    scaled = jnp.einsum(
        "ect,td->ecd", combine, cotangent.astype(f32), precision=lax.Precision.HIGHEST
    ).astype(bf16)

    def gather_rows(rows, order):
        held = rows.reshape((EXP_WIN, 1, 1, 1, 1) + rows.shape[1:])
        for name in order:
            other = swap(held, "tensor", TENSOR_MASK[name])
            dim = DIM[name] + 1
            if name in flip:
                first = jnp.where(flip[name], other, held)
                second = jnp.where(flip[name], held, other)
            else:
                first, second = held, other
            held = jnp.concatenate([first, second], axis=dim)
        return held

    def scatter_rows(rows, order):
        held = rows
        for place, name in enumerate(order):
            dim = DIM[name] + 1
            low, high = half(held, dim, 0), half(held, dim, 1)
            if name in flip:
                keep = jnp.where(flip[name], high, low)
                send = jnp.where(flip[name], low, high)
            else:
                keep, send = low, high
            held = keep.astype(f32) + swap(send.astype(bf16), "tensor", TENSOR_MASK[name]).astype(
                f32
            )
        return held.reshape((EXP_WIN,) + rows.shape[-2:])

    x_rows = gather_rows(picked, ["l", "z1", "z3", "k"])
    g_rows = gather_rows(scaled, ["z3", "l", "z1", "k"])

    def matmul(rows, weight, dims):
        return lax.dot_general(
            rows, weight, (((rows.ndim - 1,), (dims,)), ((), ())), preferred_element_type=f32
        )

    def edata_sum(rows, weight, dims, order):
        first = DIM[SPLIT[order[0]]]
        send = matmul(half(rows, first, 1), weight, dims).astype(bf16)
        other = swap(send, "edata", EDATA_MASK[order[0]])
        held = matmul(half(rows, first, 0), weight, dims).astype(bf16).astype(f32) + other.astype(
            f32
        )
        for name in order[1:]:
            dim = DIM[SPLIT[name]]
            other = swap(half(held, dim, 1).astype(bf16), "edata", EDATA_MASK[name])
            held = half(held, dim, 0) + other.astype(f32)
        return held

    def edata_gather(share, order):
        held = share
        for name in reversed(order):
            other = swap(held, "edata", EDATA_MASK[name])
            held = jnp.concatenate([held, other], axis=DIM[SPLIT[name]])
        return held

    blend_up = (0.75 * target_up.astype(f32) + 0.25 * up_weight.astype(f32)).astype(bf16)
    blend_down = (0.75 * target_down.astype(f32) + 0.25 * down_weight.astype(f32)).astype(bf16)

    pre, grad, target = {}, {}, {}
    for e in range(EXP_WIN):
        pre[e] = edata_sum(x_rows[e], up_weight[e], 0, ORDERS["pre", e])
    for e in range(EXP_WIN):
        grad[e] = edata_sum(g_rows[e], down_weight[e], 1, ORDERS["grad", e])
    for e in range(EXP_WIN):
        target[e] = edata_sum(x_rows[e], blend_up[e], 0, ORDERS["target", e])

    active, grad_pre, target_active = {}, {}, {}
    for e in range(EXP_WIN):
        active[e] = edata_gather(jax.nn.silu(pre[e]).astype(bf16), ORDERS["pre", e])
    for e in range(EXP_WIN):
        logistic = jax.nn.sigmoid(pre[e])
        value = (grad[e] * logistic * (1.0 + pre[e] * (1.0 - logistic))).astype(bf16)
        grad_pre[e] = edata_gather(value, ORDERS["grad", e])
    for e in range(EXP_WIN):
        target_active[e] = edata_gather(jax.nn.silu(target[e]).astype(bf16), ORDERS["target", e])

    def outputs(rows, weight, dims, order):
        out = jnp.stack([matmul(rows[e], weight[e], dims).astype(bf16) for e in range(EXP_WIN)])
        return combined(scatter_rows(out, order), combine)

    def weight_grad(left, right):
        def one(lhs, rhs):
            lhs = lhs.reshape(-1, lhs.shape[-1])
            rhs = rhs.reshape(-1, rhs.shape[-1])
            return lax.dot_general(
                lhs, rhs, (((0,), (0,)), ((), ())), preferred_element_type=f32
            ).astype(bf16)

        return jnp.stack([one(left[e], right[e]) for e in range(EXP_WIN)])

    mixed = outputs(active, down_weight, 0, ["k", "z3", "z1", "l"])
    grad_tokens = outputs(grad_pre, up_weight, 1, ["k", "l", "z3", "z1"])
    target_mixed = outputs(target_active, blend_down, 0, ["k", "z1", "l", "z3"])
    grad_down = weight_grad(active, g_rows)
    grad_up = weight_grad(x_rows, grad_pre)
    return (mixed, grad_tokens, grad_up, grad_down, target_mixed)


def solution(mesh):
    return jax.shard_map(
        shards,
        mesh=mesh,
        in_specs=(
            P("tensor", "edata"),
            P("tensor", None),
            P("tensor", None),
            P(None, "edata", "tensor"),
            P(None, "tensor", "edata"),
            P(None, "edata", "tensor"),
            P(None, "tensor", "edata"),
            P("tensor", "edata"),
        ),
        out_specs=(
            P("tensor", "edata"),
            P("tensor", "edata"),
            P(None, "edata", "tensor"),
            P(None, "tensor", "edata"),
            P("tensor", "edata"),
        ),
        check_vma=False,
    )
```

```python
import jax
import jax.numpy as jnp
from jax import lax
from jax.sharding import PartitionSpec as P

EXP_WIN = 2
CAP = 48

EDATA_MASK = {"a": 2, "b": 6, "c": 1}
TENSOR_MASK = {"l": 2, "z1": 4, "z3": 12, "k": 1}
DIM = {"k": 0, "z3": 1, "z1": 2, "l": 3}
SPLIT = {"a": "l", "b": "z1", "c": "z3"}
ORDERS = {
    ("pre", 0): "abc",
    ("pre", 1): "bca",
    ("target", 0): "cab",
    ("grad", 0): "bac",
    ("grad", 1): "cba",
    ("target", 1): "acb",
}


def swap(x, axis, mask):
    n = lax.axis_size(axis)
    return lax.ppermute(x, axis, [(i, i ^ mask) for i in range(n)])


def tables(expert_ids, route_weight):
    placed_list, portion_list = ([], [])
    for expert in range(EXP_WIN):
        chosen = expert_ids == expert
        listed = jnp.any(chosen, axis=1)
        position = jnp.cumsum(listed.astype(jnp.int32)) - 1
        placed = (position[None, :] == jnp.arange(CAP, dtype=jnp.int32)[:, None]) & listed[None, :]
        weight = jnp.sum(jnp.where(chosen, route_weight, 0.0), axis=1)
        placed_list.append(placed)
        portion_list.append(jnp.where(placed, weight[None, :], 0.0))
    onehot = jnp.stack(placed_list, axis=0).astype(jnp.bfloat16)
    combine = jnp.stack(portion_list, axis=0)
    return (onehot, combine)


def combined(owner_out, combine):
    return jnp.einsum("ecd,ect->td", owner_out, combine, precision=lax.Precision.HIGHEST).astype(
        jnp.bfloat16
    )


def half(x, dim, index):
    return lax.index_in_dim(x, index, dim, keepdims=True)


def shards(
    tokens, expert_ids, route_weight, up_weight, down_weight, target_up, target_down, cotangent
):
    f32, bf16 = jnp.float32, jnp.bfloat16
    index = lax.axis_index("edata")
    y, x_hi = index // 2, index % 2
    flip = {"l": ((y ^ (y // 2)) & 1) == 1, "z1": y // 2 == 1, "z3": x_hi == 1}

    onehot, combine = tables(expert_ids, route_weight)
    picked = jnp.einsum("ect,td->ecd", onehot, tokens, preferred_element_type=f32).astype(bf16)
    scaled = jnp.einsum(
        "ect,td->ecd", combine, cotangent.astype(f32), precision=lax.Precision.HIGHEST
    ).astype(bf16)

    def gather_rows(rows, order):
        held = rows.reshape((EXP_WIN, 1, 1, 1, 1) + rows.shape[1:])
        for name in order:
            other = swap(held, "tensor", TENSOR_MASK[name])
            dim = DIM[name] + 1
            if name in flip:
                first = jnp.where(flip[name], other, held)
                second = jnp.where(flip[name], held, other)
            else:
                first, second = held, other
            held = jnp.concatenate([first, second], axis=dim)
        return held

    def scatter_rows(rows, order):
        held = rows
        for place, name in enumerate(order):
            dim = DIM[name] + 1
            low, high = half(held, dim, 0), half(held, dim, 1)
            if name in flip:
                keep = jnp.where(flip[name], high, low)
                send = jnp.where(flip[name], low, high)
            else:
                keep, send = low, high
            held = keep.astype(f32) + swap(send.astype(bf16), "tensor", TENSOR_MASK[name]).astype(
                f32
            )
        return held.reshape((EXP_WIN,) + rows.shape[-2:])

    x_rows = gather_rows(picked, ["l", "z1", "z3", "k"])
    g_rows = gather_rows(scaled, ["z3", "l", "z1", "k"])

    def matmul(rows, weight, dims):
        return lax.dot_general(
            rows, weight, (((rows.ndim - 1,), (dims,)), ((), ())), preferred_element_type=f32
        )

    def edata_sum(rows, weight, dims, order):
        first = DIM[SPLIT[order[0]]]
        send = matmul(half(rows, first, 1), weight, dims).astype(bf16)
        other = swap(send, "edata", EDATA_MASK[order[0]])
        held = matmul(half(rows, first, 0), weight, dims).astype(bf16).astype(f32) + other.astype(
            f32
        )
        for name in order[1:]:
            dim = DIM[SPLIT[name]]
            other = swap(half(held, dim, 1).astype(bf16), "edata", EDATA_MASK[name])
            held = half(held, dim, 0) + other.astype(f32)
        return held

    def edata_gather(share, order):
        held = share
        for name in reversed(order):
            other = swap(held, "edata", EDATA_MASK[name])
            held = jnp.concatenate([held, other], axis=DIM[SPLIT[name]])
        return held

    blend_up = (0.75 * target_up.astype(f32) + 0.25 * up_weight.astype(f32)).astype(bf16)
    blend_down = (0.75 * target_down.astype(f32) + 0.25 * down_weight.astype(f32)).astype(bf16)

    pre, grad, target = {}, {}, {}
    for e in range(EXP_WIN):
        pre[e] = edata_sum(x_rows[e], up_weight[e], 0, ORDERS["pre", e])
    for e in range(EXP_WIN):
        grad[e] = edata_sum(g_rows[e], down_weight[e], 1, ORDERS["grad", e])
    for e in range(EXP_WIN):
        target[e] = edata_sum(x_rows[e], blend_up[e], 0, ORDERS["target", e])

    active, grad_pre, target_active = {}, {}, {}
    for e in range(EXP_WIN):
        active[e] = edata_gather(jax.nn.silu(pre[e]).astype(bf16), ORDERS["pre", e])
    for e in range(EXP_WIN):
        logistic = jax.nn.sigmoid(pre[e])
        value = (grad[e] * logistic * (1.0 + pre[e] * (1.0 - logistic))).astype(bf16)
        grad_pre[e] = edata_gather(value, ORDERS["grad", e])
    for e in range(EXP_WIN):
        target_active[e] = edata_gather(jax.nn.silu(target[e]).astype(bf16), ORDERS["target", e])

    def outputs(rows, weight, dims, order):
        out = jnp.stack([matmul(rows[e], weight[e], dims).astype(bf16) for e in range(EXP_WIN)])
        return combined(scatter_rows(out, order), combine)

    def weight_grad(left, right):
        def one(lhs, rhs):
            lhs = lhs.reshape(-1, lhs.shape[-1])
            rhs = rhs.reshape(-1, rhs.shape[-1])
            return lax.dot_general(
                lhs, rhs, (((0,), (0,)), ((), ())), preferred_element_type=f32
            ).astype(bf16)

        return jnp.stack([one(left[e], right[e]) for e in range(EXP_WIN)])

    mixed = outputs(active, down_weight, 0, ["k", "z3", "z1", "l"])
    grad_tokens = outputs(grad_pre, up_weight, 1, ["k", "l", "z3", "z1"])
    target_mixed = outputs(target_active, blend_down, 0, ["k", "z1", "l", "z3"])
    grad_down = weight_grad(active, g_rows)
    grad_up = weight_grad(x_rows, grad_pre)
    return (mixed, grad_tokens, grad_up, grad_down, target_mixed)


def solution(mesh):
    return jax.shard_map(
        shards,
        mesh=mesh,
        in_specs=(
            P("tensor", "edata"),
            P("tensor", None),
            P("tensor", None),
            P(None, "edata", "tensor"),
            P(None, "tensor", "edata"),
            P(None, "edata", "tensor"),
            P(None, "tensor", "edata"),
            P("tensor", "edata"),
        ),
        out_specs=(
            P("tensor", "edata"),
            P("tensor", "edata"),
            P(None, "edata", "tensor"),
            P(None, "tensor", "edata"),
            P("tensor", "edata"),
        ),
        check_vma=False,
    )
```
